256 devices in a mesh: radial: 16 (over x_lo, z), axial: 16 (over y, x_hi, core).
Axes of the slice: x: 4 (x_hi: 2, x_lo: 2; x = x_hi * 2 + x_lo), y: 4, z: 8, core: 2. Of those that a mesh axis runs over, the one named last changes fastest.
Arguments:
- responses: bfloat16 [16, 16, 2, 256, 256], P('radial', 'axial'), may hold values from -6 to 6
- owners: int32 [2], replicated, may hold values from 0 to 255
- panel: bfloat16 [16, 16, 12288, 256], P('radial', 'axial'), may hold values from -0.375 to 0.375
- node_map: int32 [16, 16, 12288], P('radial', 'axial'), may hold values from 0 to 12287, each once within a row
- modulus: float32 [128, 128, 64], P('radial', 'axial'), may hold values from 0.5 to 5
Outputs:
- equivalent_stress: bfloat16 [128, 128, 64, 512], P('radial', 'axial')
The draws below stay inside these ranges and needn't reach their ends.
Inputs may be any that keep to these rules, and one draw needn't show every extreme that they name: Each tile's node_map holds every panel row 0 to 12287 exactly once.
All inputs are finite; a program needn't handle non-finite values.
Results may differ from the reference program's by a relative error of at most 0.0034.
Values may be sent and summed in bfloat16 or wider, within the bound.
No kernel may reach another device: no remote copies, remote signals or barrier semaphores. Data moves between devices by JAX's collectives and lax.ppermute only.
A program may use at most 192 MiB of HBM per device.

```python
import math
import jax
import jax.numpy as jnp
from jax import lax

MODES = 256
TIMES = 256
HARM = 2
RN = 8
AN = 8
CN = 64
DOF_DEV = 12288
NR = 128
NA = 128
N_RADIAL = 16
N_AXIAL = 16
DEVICES = 256


def level_of(stream_key, shape, split, smallest, top_value):
    gain, own = 1.0, jax.random.fold_in(stream_key, 6)
    for dim, parts in split:
        heights = jnp.exp(jax.random.uniform(jax.random.fold_in(own, dim), (parts,), jnp.float32, smallest / len(split), top_value / len(split)))
        gain = gain * jnp.repeat(heights, shape[dim] // parts).reshape([-1 if axis == dim else 1 for axis in range(len(shape))])
    return gain


def centred(stream_key, dims, spread, limit, shards=(), dtype=jnp.bfloat16):
    level = level_of(stream_key, dims, shards, -0.22, 0.18) if shards else 1.0
    array = jax.random.normal(stream_key, dims, jnp.float32) * spread * level
    return jnp.minimum(jnp.maximum(array, -limit), limit).astype(dtype)


def setup_inputs(seed: int = 0) -> dict:
    key_list = jax.random.split(jax.random.key(seed), 6)
    responses = centred(key_list[0], (N_RADIAL, N_AXIAL, HARM, MODES, TIMES), 1.0, 6.0, ((0, 16), (1, 16)))
    owners = jax.random.randint(key_list[1], (HARM,), 0, DEVICES).astype(jnp.int32)
    panel = centred(key_list[2], (N_RADIAL, N_AXIAL, DOF_DEV, MODES), MODES ** -0.5, 0.375, ((0, 16), (1, 16)))
    node_map = jax.vmap(lambda own: jax.random.permutation(own, DOF_DEV))(jax.random.split(key_list[3], N_RADIAL * N_AXIAL)).reshape((N_RADIAL, N_AXIAL, DOF_DEV)).astype(jnp.int32)
    modulus = jnp.clip(jnp.exp(math.log(5.0) - 2.3025851 * jax.random.uniform(key_list[4], (NR, NA, CN), jnp.float32) ** level_of(key_list[4], (NR, NA, CN), ((0, 16), (1, 16)), -0.2, 0.2)), 0.5, 5.0)
    return {"responses": responses, "owners": owners, "panel": panel, "node_map": node_map, "modulus": modulus}


poisson = 0.3

def stress_block(padded, modulus):
    field = jnp.pad(padded.astype(jnp.float32), ((0, 0), (0, 0), (0, 0), (1, 1), (0, 0)))
    derivs = [0.5 * (field[:, 2:, 1:-1, 1:-1] - field[:, :-2, 1:-1, 1:-1]), 0.5 * (field[:, 1:-1, 2:, 1:-1] - field[:, 1:-1, :-2, 1:-1]), 0.5 * (field[:, 1:-1, 1:-1, 2:] - field[:, 1:-1, 1:-1, :-2])]
    strain = [[0.5 * (derivs[second][first] + derivs[first][second]) for second in range(3)] for first in range(3)]
    elastic = modulus[..., None]
    shear = elastic / (2.0 * (1.0 + poisson))
    lame = elastic * poisson / ((1.0 + poisson) * (1.0 - 2.0 * poisson))
    volume = strain[0][0] + strain[1][1] + strain[2][2]
    normal_s = [lame * volume + 2.0 * shear * strain[first][first] for first in range(3)]
    shear_s = [2.0 * shear * strain[0][1], 2.0 * shear * strain[1][2], 2.0 * shear * strain[0][2]]
    mises = 0.5 * ((normal_s[0] - normal_s[1]) ** 2 + (normal_s[1] - normal_s[2]) ** 2 + (normal_s[2] - normal_s[0]) ** 2)
    mises = mises + 3.0 * (shear_s[0] ** 2 + shear_s[1] ** 2 + shear_s[2] ** 2)
    return jnp.sqrt(mises)

def von_mises(padded, modulus):
    width = padded.shape[-1]
    block_count = width // 128

    def one_block(start):
        piece = lax.dynamic_slice_in_dim(padded, start, 128, 4)
        return stress_block(piece, modulus)
    starts = (jnp.arange(block_count) * 128).astype(jnp.int32)
    stacked = lax.map(one_block, starts)
    shape = stacked.shape
    return jnp.moveaxis(stacked, 0, 3).reshape(shape[1], shape[2], shape[3], width).astype(jnp.bfloat16)

def expand_tile(panel_tile, map_tile, modal):
    ordered = panel_tile[map_tile]
    return jnp.dot(ordered, modal, preferred_element_type=jnp.float32).astype(jnp.bfloat16)

def reference(responses, owners, panel, node_map, modulus):
    flat = responses.reshape((-1,) + responses.shape[2:])
    modal = jnp.concatenate([flat[owners[harmonic], harmonic] for harmonic in range(HARM)], axis=1)
    width = HARM * TIMES

    def expand_row(index):
        tiles = lax.map(lambda pair: expand_tile(pair[0], pair[1], modal), (panel[index], node_map[index]))
        tiles = tiles.reshape(N_AXIAL, 3, RN, AN, CN, width)
        return jnp.moveaxis(tiles, 0, 2).reshape(3, RN, N_AXIAL * AN, CN, width)
    first_row = expand_row(jnp.int32(0))
    zero_row = jnp.zeros_like(first_row)

    def step(carry, index):
        before, current = carry
        later = expand_row(jnp.minimum(index + 1, N_RADIAL - 1).astype(jnp.int32))
        later = jnp.where(index + 1 < N_RADIAL, later, zero_row)
        padded = jnp.concatenate([before[:, -1:], current, later[:, :1]], axis=1)
        padded = jnp.pad(padded, ((0, 0), (0, 0), (1, 1), (0, 0), (0, 0)))
        row_modulus = lax.dynamic_slice_in_dim(modulus, (index * RN).astype(jnp.int32), RN, 0)
        return ((current, later), von_mises(padded, row_modulus))
    unused, stress_rows = lax.scan(step, (zero_row, first_row), jnp.arange(N_RADIAL).astype(jnp.int32))
    return stress_rows.reshape(NR, NA, CN, width)
```

```python
import math

import jax
import jax.numpy as jnp
from jax import lax
from jax.experimental import pallas as pl
from jax.experimental.pallas import tpu as pltpu
from jax.sharding import PartitionSpec as P

RN = 8
AN = 8
CN = 64
ROWS = 3 * CN
AXES = ("radial", "axial")
POISSON = 0.3
LAME_RATIO = POISSON / (1.0 - 2.0 * POISSON)
SCALE = math.sqrt(0.5) / (2.0 * (1.0 + POISSON))
TINY = 1.1754944e-38


def swapped(kind, mask):
    pairs = []
    for i in range(256):
        radial, axial = divmod(i, 16)
        x, z = (axial // 2) % 2 * 2 + radial // 8, radial % 8
        y, core = axial // 4, axial % 2
        if kind == "core":
            core ^= mask
        elif kind == "z":
            z ^= mask
        elif kind == "y":
            y ^= mask
        else:
            x ^= mask
        pairs.append((i, (x % 2 * 8 + z) * 16 + y * 4 + x // 2 * 2 + core))
    return pairs


def sent(value, kind, mask):
    return lax.ppermute(value, AXES, swapped(kind, mask))


ROUNDS = (("x", 1), ("x", 3), ("y", 1), ("y", 3), ("z", 1), ("z", 2), ("z", 6))


def broadcast(responses, owners, work):
    work = list(work)

    def round_of(value, kind, mask):
        value = lax.optimization_barrier(value)
        part = sent(value, kind, mask)
        done = work.pop(0)(value) if work else ()
        return lax.optimization_barrier((part, done))[0]

    me = lax.axis_index(AXES)
    core = me % 2
    first, second = (
        jnp.where(me == owners[h], responses[0, 0, h], 0).astype(responses.dtype) for h in range(2)
    )
    held = jnp.where(core == 0, first, second)
    held = held + round_of(jnp.where(core == 0, second, first), "core", 1)
    for kind, mask in ROUNDS:
        held = held + round_of(held, kind, mask)
    return held, round_of(held, "core", 1)


def gathered(node_map, panel, groups, name):
    total = panel.shape[0]

    def kernel(map_ref, panel_ref, *refs):
        out_refs, (wide, buf) = refs[: len(groups)], refs[len(groups) :]

        def widen(j, _):
            start = pl.multiple_of(j * 64, 64)
            value = panel_ref[pl.ds(start, 64), :].astype(jnp.float32)
            to = pl.multiple_of(2 * start, 128)
            wide[pl.ds(to, 64, stride=2), :] = value[:, :128]
            wide[pl.ds(to + 1, 64, stride=2), :] = value[:, 128:]
            return 0

        lax.fori_loop(0, total // 64, widen, 0, unroll=4)

        for (count, column), out_ref in zip(groups, out_refs):

            def pair(p, _, column=column, out_ref=out_ref):
                def run(j, _):
                    radial, axial = column(2 * p + j // 3)
                    base = ((j % 3 * RN + radial) * AN + axial) * CN
                    rows = []
                    for i in range(CN):
                        row = map_ref[base + i]
                        rows.append(wide[pl.ds(pl.multiple_of(2 * row, 2), 2), :])
                    to = pl.multiple_of(j * 2 * CN, 2 * CN)
                    for i in range(CN):
                        buf[pl.ds(to + 2 * i, 2), :] = rows[i]
                    return 0

                lax.fori_loop(0, 6, run, 0)
                start = pl.multiple_of(p * 2 * ROWS, 2 * ROWS)
                for half in range(2):
                    out_ref[pl.ds(start, 2 * ROWS), half * 128 : half * 128 + 128] = buf[
                        pl.ds(half, 2 * ROWS, stride=2), :
                    ].astype(jnp.bfloat16)
                return 0

            lax.fori_loop(0, count // 2, pair, 0)

    vmem = pl.BlockSpec(memory_space=pltpu.VMEM)
    return pl.pallas_call(
        kernel,
        in_specs=[pl.BlockSpec(memory_space=pltpu.SMEM), vmem],
        out_specs=[vmem] * len(groups),
        out_shape=[jax.ShapeDtypeStruct((n * ROWS, 256), jnp.bfloat16) for n, _ in groups],
        scratch_shapes=[
            pltpu.VMEM((2 * total, 128), jnp.float32),
            pltpu.VMEM((4 * ROWS, 128), jnp.float32),
        ],
        compiler_params=pltpu.CompilerParams(vmem_limit_bytes=16 << 20),
        cost_estimate=pl.CostEstimate(flops=0, transcendentals=0, bytes_accessed=0),
        name=name,
    )(node_map, panel)


def stressed(halos, faces, inner, modal, core, scale):
    def kernel(*refs):
        halo_refs, face_refs, inner_refs = refs[:4], refs[4:8], refs[8:11]
        held_ref, other_ref, core_ref, scale_ref, out_ref, modal_ref, field = refs[11:]
        harmonic, radial = pl.program_id(0), pl.program_id(1)

        def displace(ref, first, count, place):
            for start in range(first, first + count, 4):
                n = min(4, first + count - start)
                value = jnp.dot(
                    ref[start * ROWS : (start + n) * ROWS, :],
                    modal_ref[harmonic],
                    preferred_element_type=jnp.float32,
                )
                value = value.astype(jnp.bfloat16).astype(jnp.float32)
                for b in range(n):
                    r, a = place(start + b)
                    for k in range(3):
                        low = b * ROWS + k * CN
                        for t in range(2):
                            field[r, a, k, t, 8 : 8 + CN, :] = value[
                                low : low + CN, t * 128 : t * 128 + 128
                            ]

        @pl.when(jnp.logical_and(radial == 0, harmonic == 0))
        def _():
            core = core_ref[0]
            modal_ref[core] = held_ref[...]
            modal_ref[1 - core] = other_ref[...]
            zeros = jnp.zeros((8, 128), jnp.float32)

            def clear(r, _):
                for a in range(1, AN + 1):
                    for k in range(3):
                        for t in range(2):
                            field[r, a, k, t, 0:8, :] = zeros
                            field[r, a, k, t, 8 + CN : 16 + CN, :] = zeros
                return 0

            lax.fori_loop(0, 3, clear, 0)

        def slab(s):
            if s == 0:
                displace(halo_refs[0], 0, 8, lambda b: (s % 3, b + 1))
            elif s == RN + 1:
                displace(halo_refs[1], 0, 8, lambda b: (s % 3, b + 1))
            else:
                displace(halo_refs[2], s - 1, 1, lambda b: (s % 3, 0))
                displace(halo_refs[3], s - 1, 1, lambda b: (s % 3, AN + 1))
                if s == 1 or s == RN:
                    displace(face_refs[s // RN], 0, 8, lambda b: (s % 3, b + 1))
                else:
                    displace(face_refs[2], s - 1, 1, lambda b: (s % 3, 1))
                    displace(face_refs[3], s - 1, 1, lambda b: (s % 3, AN))
                    part, place = divmod(s - 2, 2)
                    skip = (AN - 2) * place
                    displace(inner_refs[part], skip, 6, lambda b: (s % 3, b - skip + 2))

        @pl.when(radial == 0)
        def _():
            slab(0)
            slab(1)

        for s in range(2, RN + 2):
            pl.when(radial == s - 2)(lambda s=s: slab(s))
        low, mid, high = (lax.rem(radial + i, 3) for i in range(3))

        for a in range(AN):
            for start in range(0, CN, 16):
                factor = jnp.broadcast_to(
                    scale_ref[radial, start : start + 16, a : a + 1], (16, 128)
                )
                here = slice(8 + start, 24 + start)
                after = slice(9 + start, 25 + start)
                before = slice(7 + start, 23 + start)
                for t in range(2):
                    diff = [
                        [
                            field[high, a + 1, k, t, here, :]
                            - field[low, a + 1, k, t, here, :],
                            field[mid, a + 2, k, t, here, :]
                            - field[mid, a, k, t, here, :],
                            field[mid, a + 1, k, t, after, :]
                            - field[mid, a + 1, k, t, before, :],
                        ]
                        for k in range(3)
                    ]
                    volume = (diff[0][0] + diff[1][1] + diff[2][2]) * LAME_RATIO
                    normal = [volume + diff[k][k] for k in range(3)]
                    total = (
                        (normal[0] - normal[1]) ** 2
                        + (normal[1] - normal[2]) ** 2
                        + (normal[2] - normal[0]) ** 2
                    )
                    mixed = (
                        (diff[0][1] + diff[1][0]) ** 2
                        + (diff[1][2] + diff[2][1]) ** 2
                        + (diff[0][2] + diff[2][0]) ** 2
                    )
                    total = total + 1.5 * mixed
                    root = total * lax.rsqrt(jnp.maximum(total, TINY))
                    out_ref[0, a, start : start + 16, t * 128 : t * 128 + 128] = (
                        factor * root
                    ).astype(jnp.bfloat16)

    vmem = pl.BlockSpec(memory_space=pltpu.VMEM)
    return pl.pallas_call(
        kernel,
        grid=(2, RN),
        in_specs=[vmem] * 13
        + [
            pl.BlockSpec(memory_space=pltpu.SMEM),
            pl.BlockSpec((RN, CN, AN), lambda h, r: (0, 0, 0)),
        ],
        out_specs=pl.BlockSpec((1, AN, CN, 256), lambda h, r: (r, 0, 0, h)),
        out_shape=jax.ShapeDtypeStruct((RN, AN, CN, 512), jnp.bfloat16),
        scratch_shapes=[
            pltpu.VMEM((2, 256, 256), jnp.bfloat16),
            pltpu.VMEM((3, AN + 2, 3, 2, CN + 16, 128), jnp.float32),
        ],
        compiler_params=pltpu.CompilerParams(vmem_limit_bytes=16 << 20),
        name="stress",
    )(*halos, *faces, *inner, *modal, core, scale)


def local(responses, owners, panel, node_map, modulus):
    last_r, last_a, span = RN - 1, AN - 1, AN - 2
    up = [(i, i + 1) for i in range(15)]
    down = [(i + 1, i) for i in range(15)]
    faces, inner = [], []

    def rows(value, groups, name):
        own = lax.optimization_barrier((node_map[0, 0], value))[0]
        return gathered(own, panel[0, 0], groups, name)

    def face(column, name):
        def run(value):
            faces.extend(rows(value, [(8, column)], name))
            return (faces[-1],)

        return run

    def inner_rows(part):
        def run(value):
            groups = [(2 * span, lambda b: (1 + 2 * part + b // span, 1 + b % span))]
            inner.extend(rows(value, groups, f"rows_inner_{part}"))
            return (inner[-1],)

        return run

    modal = broadcast(
        responses,
        owners,
        [
            face(lambda b: (0, b), "rows_r0"),
            face(lambda b: (last_r, b), "rows_r7"),
            face(lambda b: (b, 0), "rows_a0"),
            face(lambda b: (b, last_a), "rows_a7"),
            inner_rows(0),
            inner_rows(1),
            inner_rows(2),
        ],
    )
    halos = [
        lax.ppermute(faces[1], "radial", up),
        lax.ppermute(faces[0], "radial", down),
        lax.ppermute(faces[3], "axial", up),
        lax.ppermute(faces[2], "axial", down),
    ]
    core = jnp.reshape(lax.axis_index(AXES) % 2, (1,)).astype(jnp.int32)
    scale = jnp.transpose(modulus * SCALE, (0, 2, 1))
    return stressed(halos, faces, inner, modal, core, scale)


def solution(mesh):
    return jax.shard_map(
        local,
        mesh=mesh,
        in_specs=(
            P("radial", "axial", None, None, None),
            P(),
            P("radial", "axial", None, None),
            P("radial", "axial", None),
            P("radial", "axial", None),
        ),
        out_specs=P("radial", "axial", None, None),
        check_vma=False,
    )
```

```python
import math

import jax
import jax.numpy as jnp
from jax import lax
from jax.experimental import pallas as pl
from jax.experimental.pallas import tpu as pltpu
from jax.sharding import PartitionSpec as P

RN = 8
AN = 8
CN = 64
ROWS = 3 * CN
AXES = ("radial", "axial")
POISSON = 0.3
LAME_RATIO = POISSON / (1.0 - 2.0 * POISSON)
SCALE = math.sqrt(0.5) / (2.0 * (1.0 + POISSON))
TINY = 1.1754944e-38


def swapped(kind, mask):
    pairs = []
    for i in range(256):
        radial, axial = divmod(i, 16)
        x, z = (axial // 2) % 2 * 2 + radial // 8, radial % 8
        y, core = axial // 4, axial % 2
        if kind == "core":
            core ^= mask
        elif kind == "z":
            z ^= mask
        elif kind == "y":
            y ^= mask
        else:
            x ^= mask
        pairs.append((i, (x % 2 * 8 + z) * 16 + y * 4 + x // 2 * 2 + core))
    return pairs


def sent(value, kind, mask):
    return lax.ppermute(value, AXES, swapped(kind, mask))


def added(a, b):
    def kernel(a_ref, b_ref, out_ref):
        out_ref[...] = a_ref[...] + b_ref[...]

    vmem = pl.BlockSpec(memory_space=pltpu.VMEM)
    return pl.pallas_call(
        kernel,
        in_specs=[vmem, vmem],
        out_specs=vmem,
        out_shape=jax.ShapeDtypeStruct(a.shape, a.dtype),
        compiler_params=pltpu.CompilerParams(vmem_limit_bytes=1 << 20),
        cost_estimate=pl.CostEstimate(flops=0, transcendentals=0, bytes_accessed=0),
        name="add",
    )(a, b)


def masked(responses, owners, me, core):
    def kernel(owners_ref, place_ref, in_ref, own_ref, other_ref):
        me, core = place_ref[0], place_ref[1]
        for out_ref, h in ((own_ref, core), (other_ref, 1 - core)):

            @pl.when(owners_ref[h] == me)
            def _(out_ref=out_ref, h=h):
                out_ref[...] = in_ref[h]

            @pl.when(owners_ref[h] != me)
            def _(out_ref=out_ref):
                out_ref[...] = jnp.zeros_like(out_ref)

    smem, vmem = pl.BlockSpec(memory_space=pltpu.SMEM), pl.BlockSpec(memory_space=pltpu.VMEM)
    shape = jax.ShapeDtypeStruct(responses.shape[1:], responses.dtype)
    return pl.pallas_call(
        kernel,
        in_specs=[smem, smem, vmem],
        out_specs=[vmem, vmem],
        out_shape=[shape, shape],
        compiler_params=pltpu.CompilerParams(vmem_limit_bytes=1 << 20),
        name="mask",
    )(owners, jnp.stack([me, core]).astype(jnp.int32), responses)


ROUNDS = (("x", 1), ("x", 3), ("y", 1), ("y", 3), ("z", 1), ("z", 2), ("z", 6))


def broadcast(responses, owners, work):
    work = list(work)

    def round_of(value, kind, mask):
        value = lax.optimization_barrier(value)
        part = sent(value, kind, mask)
        done = work.pop(0)(value) if work else ()
        return lax.optimization_barrier((part, done))[0]

    me = lax.axis_index(AXES)
    core = me % 2
    held, other = masked(responses[0, 0], owners, me, core)
    held = added(held, round_of(other, "core", 1))
    for kind, mask in ROUNDS:
        held = added(held, round_of(held, kind, mask))
    return held, round_of(held, "core", 1)


def widened(panel):
    total = panel.shape[0]

    def kernel(panel_ref, wide_ref):
        def widen(j, _):
            start = pl.multiple_of(j * 64, 64)
            value = panel_ref[pl.ds(start, 64), :].astype(jnp.float32)
            to = pl.multiple_of(2 * start, 128)
            wide_ref[pl.ds(to, 64, stride=2), :] = value[:, :128]
            wide_ref[pl.ds(to + 1, 64, stride=2), :] = value[:, 128:]
            return 0

        lax.fori_loop(0, total // 64, widen, 0, unroll=4)

    vmem = pl.BlockSpec(memory_space=pltpu.VMEM)
    return pl.pallas_call(
        kernel,
        in_specs=[vmem],
        out_specs=vmem,
        out_shape=pltpu.VMEM((2 * total, 128), jnp.float32),
        compiler_params=pltpu.CompilerParams(vmem_limit_bytes=1 << 20),
        cost_estimate=pl.CostEstimate(flops=0, transcendentals=0, bytes_accessed=0),
        name="widen",
    )(panel)


def gathered(node_map, wide, count, column, name):
    def kernel(map_ref, wide_ref, out_ref, _, buf):
        def pair(p, _):
            def run(j, _):
                radial, axial = column(2 * p + j // 3)
                base = ((j % 3 * RN + radial) * AN + axial) * CN
                rows = []
                for i in range(CN):
                    row = map_ref[base + i]
                    rows.append(wide_ref[pl.ds(pl.multiple_of(2 * row, 2), 2), :])
                to = pl.multiple_of(j * 2 * CN, 2 * CN)
                for i in range(CN):
                    buf[pl.ds(to + 2 * i, 2), :] = rows[i]
                return 0

            lax.fori_loop(0, 6, run, 0)
            start = pl.multiple_of(p * 2 * ROWS, 2 * ROWS)
            for half in range(2):
                out_ref[pl.ds(start, 2 * ROWS), half * 128 : half * 128 + 128] = buf[
                    pl.ds(half, 2 * ROWS, stride=2), :
                ].astype(jnp.bfloat16)
            return 0

        lax.fori_loop(0, count // 2, pair, 0)

    vmem = pl.BlockSpec(memory_space=pltpu.VMEM)
    return pl.pallas_call(
        kernel,
        in_specs=[pl.BlockSpec(memory_space=pltpu.SMEM), vmem],
        out_specs=[vmem, vmem],
        out_shape=[
            jax.ShapeDtypeStruct((count * ROWS, 256), jnp.bfloat16),
            pltpu.VMEM(wide.shape, wide.dtype),
        ],
        input_output_aliases={1: 1},
        scratch_shapes=[pltpu.VMEM((4 * ROWS, 128), jnp.float32)],
        compiler_params=pltpu.CompilerParams(vmem_limit_bytes=2 << 20),
        cost_estimate=pl.CostEstimate(flops=0, transcendentals=0, bytes_accessed=0),
        name=name,
    )(node_map, wide)


def stressed(halos, faces, inner, modal, core, modulus):
    def kernel(*refs):
        halo_refs, face_refs, inner_refs = refs[:4], refs[4:8], refs[8:11]
        held_ref, other_ref, core_ref, modulus_ref, out_ref, modal_ref, field = refs[11:]
        harmonic, radial = pl.program_id(0), pl.program_id(1)

        def displace(ref, first, count, place):
            for start in range(first, first + count, 4):
                n = min(4, first + count - start)
                value = jnp.dot(
                    ref[start * ROWS : (start + n) * ROWS, :],
                    modal_ref[harmonic],
                    preferred_element_type=jnp.float32,
                )
                value = value.astype(jnp.bfloat16).astype(jnp.float32)
                for b in range(n):
                    r, a = place(start + b)
                    for k in range(3):
                        low = b * ROWS + k * CN
                        for t in range(2):
                            field[r, a, k, t, 8 : 8 + CN, :] = value[
                                low : low + CN, t * 128 : t * 128 + 128
                            ]

        @pl.when(jnp.logical_and(radial == 0, harmonic == 0))
        def _():
            core = core_ref[0]
            modal_ref[core] = held_ref[...]
            modal_ref[1 - core] = other_ref[...]
            zeros = jnp.zeros((8, 128), jnp.float32)

            def clear(r, _):
                for a in range(1, AN + 1):
                    for k in range(3):
                        for t in range(2):
                            field[r, a, k, t, 0:8, :] = zeros
                            field[r, a, k, t, 8 + CN : 16 + CN, :] = zeros
                return 0

            lax.fori_loop(0, 3, clear, 0)

        def slab(s):
            if s == 0:
                displace(halo_refs[0], 0, 8, lambda b: (s % 3, b + 1))
            elif s == RN + 1:
                displace(halo_refs[1], 0, 8, lambda b: (s % 3, b + 1))
            else:
                displace(halo_refs[2], s - 1, 1, lambda b: (s % 3, 0))
                displace(halo_refs[3], s - 1, 1, lambda b: (s % 3, AN + 1))
                if s == 1 or s == RN:
                    displace(face_refs[s // RN], 0, 8, lambda b: (s % 3, b + 1))
                else:
                    displace(face_refs[2], s - 1, 1, lambda b: (s % 3, 1))
                    displace(face_refs[3], s - 1, 1, lambda b: (s % 3, AN))
                    part, place = divmod(s - 2, 2)
                    skip = (AN - 2) * place
                    displace(inner_refs[part], skip, 6, lambda b: (s % 3, b - skip + 2))

        @pl.when(radial == 0)
        def _():
            slab(0)
            slab(1)

        for s in range(2, RN + 2):
            pl.when(radial == s - 2)(lambda s=s: slab(s))
        low, mid, high = (lax.rem(radial + i, 3) for i in range(3))

        scale = jnp.transpose(modulus_ref[0] * SCALE)
        for a in range(AN):
            for start in range(0, CN, 16):
                factor = jnp.broadcast_to(scale[start : start + 16, a : a + 1], (16, 128))
                here = slice(8 + start, 24 + start)
                after = slice(9 + start, 25 + start)
                before = slice(7 + start, 23 + start)
                for t in range(2):
                    diff = [
                        [
                            field[high, a + 1, k, t, here, :]
                            - field[low, a + 1, k, t, here, :],
                            field[mid, a + 2, k, t, here, :]
                            - field[mid, a, k, t, here, :],
                            field[mid, a + 1, k, t, after, :]
                            - field[mid, a + 1, k, t, before, :],
                        ]
                        for k in range(3)
                    ]
                    volume = (diff[0][0] + diff[1][1] + diff[2][2]) * LAME_RATIO
                    normal = [volume + diff[k][k] for k in range(3)]
                    total = (
                        (normal[0] - normal[1]) ** 2
                        + (normal[1] - normal[2]) ** 2
                        + (normal[2] - normal[0]) ** 2
                    )
                    mixed = (
                        (diff[0][1] + diff[1][0]) ** 2
                        + (diff[1][2] + diff[2][1]) ** 2
                        + (diff[0][2] + diff[2][0]) ** 2
                    )
                    total = total + 1.5 * mixed
                    root = total * lax.rsqrt(jnp.maximum(total, TINY))
                    out_ref[0, a, start : start + 16, t * 128 : t * 128 + 128] = (
                        factor * root
                    ).astype(jnp.bfloat16)

    vmem = pl.BlockSpec(memory_space=pltpu.VMEM)
    return pl.pallas_call(
        kernel,
        grid=(2, RN),
        in_specs=[vmem] * 13
        + [
            pl.BlockSpec(memory_space=pltpu.SMEM),
            pl.BlockSpec((1, AN, CN), lambda h, r: (r, 0, 0)),
        ],
        out_specs=pl.BlockSpec((1, AN, CN, 256), lambda h, r: (r, 0, 0, h)),
        out_shape=jax.ShapeDtypeStruct((RN, AN, CN, 512), jnp.bfloat16),
        scratch_shapes=[
            pltpu.VMEM((2, 256, 256), jnp.bfloat16),
            pltpu.VMEM((3, AN + 2, 3, 2, CN + 16, 128), jnp.float32),
        ],
        compiler_params=pltpu.CompilerParams(vmem_limit_bytes=16 << 20),
        name="stress",
    )(*halos, *faces, *inner, *modal, core, modulus)


def local(responses, owners, panel, node_map, modulus):
    last_r, last_a, span = RN - 1, AN - 1, AN - 2
    up = [(i, i + 1) for i in range(15)]
    down = [(i + 1, i) for i in range(15)]
    columns = {
        "rows_r0": (8, lambda b: (0, b)),
        "rows_r7": (8, lambda b: (last_r, b)),
        "rows_a0": (8, lambda b: (b, 0)),
        "rows_a7": (8, lambda b: (b, last_a)),
    }
    for part in range(3):
        columns[f"rows_inner_{part}"] = (
            2 * span,
            lambda b, part=part: (1 + 2 * part + b // span, 1 + b % span),
        )
    wide, rows = [], {}

    def gather(*names):
        def run(value):
            if not wide:
                wide.append(widened(lax.optimization_barrier((panel[0, 0], value))[0]))
            own = lax.optimization_barrier((node_map[0, 0], value))[0]
            for name in names:
                rows[name], wide[0] = gathered(own, wide[0], *columns[name], name)
            return tuple(rows[name] for name in names)

        return run

    modal = broadcast(
        responses,
        owners,
        [
            gather("rows_r0"),
            gather("rows_r7", "rows_a0"),
            gather("rows_a7"),
            gather("rows_inner_0"),
            gather("rows_inner_1"),
            gather("rows_inner_2"),
        ],
    )
    halos = [
        lax.ppermute(rows["rows_r7"], "radial", up),
        lax.ppermute(rows["rows_r0"], "radial", down),
        lax.ppermute(rows["rows_a7"], "axial", up),
        lax.ppermute(rows["rows_a0"], "axial", down),
    ]
    core = jnp.reshape(lax.axis_index(AXES) % 2, (1,)).astype(jnp.int32)
    faces = [rows[name] for name in ("rows_r0", "rows_r7", "rows_a0", "rows_a7")]
    inner = [rows[f"rows_inner_{part}"] for part in range(3)]
    return stressed(halos, faces, inner, modal, core, modulus)


def solution(mesh):
    return jax.shard_map(
        local,
        mesh=mesh,
        in_specs=(
            P("radial", "axial", None, None, None),
            P(),
            P("radial", "axial", None, None),
            P("radial", "axial", None),
            P("radial", "axial", None),
        ),
        out_specs=P("radial", "axial", None, None),
        check_vma=False,
    )
```

```python
import math

import jax
import jax.numpy as jnp
from jax import lax
from jax.experimental import pallas as pl
from jax.experimental.pallas import tpu as pltpu
from jax.sharding import PartitionSpec as P

RN = 8
AN = 8
CN = 64
ROWS = 3 * CN
AXES = ("radial", "axial")
POISSON = 0.3
LAME_RATIO = POISSON / (1.0 - 2.0 * POISSON)
SCALE = math.sqrt(0.5) / (2.0 * (1.0 + POISSON))
TINY = 1.1754944e-38


def swapped(kind, mask):
    pairs = []
    for i in range(256):
        radial, axial = divmod(i, 16)
        x, z = (axial // 2) % 2 * 2 + radial // 8, radial % 8
        y, core = axial // 4, axial % 2
        if kind == "core":
            core ^= mask
        elif kind == "z":
            z ^= mask
        elif kind == "y":
            y ^= mask
        else:
            x ^= mask
        pairs.append((i, (x % 2 * 8 + z) * 16 + y * 4 + x // 2 * 2 + core))
    return pairs


def sent(value, kind, mask):
    return lax.ppermute(value, AXES, swapped(kind, mask))


WORK = (
    ("radial_b",),
    ("radial_a",),
    ("axial_b",),
    ("axial_a",),
    ("inner_0",),
    ("inner_1",),
    ("inner_2",),
)


def added(a, b):
    def kernel(a_ref, b_ref, out_ref):
        out_ref[...] = a_ref[...] + b_ref[...]

    vmem = pl.BlockSpec(memory_space=pltpu.VMEM)
    return pl.pallas_call(
        kernel,
        in_specs=[vmem, vmem],
        out_specs=vmem,
        out_shape=jax.ShapeDtypeStruct(a.shape, a.dtype),
        compiler_params=pltpu.CompilerParams(vmem_limit_bytes=1 << 20),
        cost_estimate=pl.CostEstimate(flops=0, transcendentals=0, bytes_accessed=0),
        name="add",
    )(a, b)


def masked(responses, owners, place):
    def kernel(owners_ref, place_ref, in_ref, own_ref, other_ref):
        me, core = place_ref[0], place_ref[1]
        for out_ref, h in ((own_ref, core), (other_ref, 1 - core)):

            @pl.when(owners_ref[h] == me)
            def _(out_ref=out_ref, h=h):
                out_ref[...] = in_ref[h]

            @pl.when(owners_ref[h] != me)
            def _(out_ref=out_ref):
                out_ref[...] = jnp.zeros_like(out_ref)

    smem, vmem = pl.BlockSpec(memory_space=pltpu.SMEM), pl.BlockSpec(memory_space=pltpu.VMEM)
    shape = jax.ShapeDtypeStruct(responses.shape[1:], responses.dtype)
    return pl.pallas_call(
        kernel,
        in_specs=[smem, smem, vmem],
        out_specs=[vmem, vmem],
        out_shape=[shape, shape],
        compiler_params=pltpu.CompilerParams(vmem_limit_bytes=1 << 20),
        name="mask",
    )(owners, place, responses)


ROUNDS = (("x", 1), ("x", 3), ("y", 1), ("y", 3), ("z", 1), ("z", 2), ("z", 6))


def broadcast(responses, owners, place, work):
    work = list(work)

    def round_of(value, kind, mask):
        value = lax.optimization_barrier(value)
        part = sent(value, kind, mask)
        done = work.pop(0)(value) if work else ()
        return lax.optimization_barrier((part, done))[0]

    held, other = masked(responses[0, 0], owners, place)
    held = added(held, round_of(other, "core", 1))
    for kind, mask in ROUNDS:
        held = added(held, round_of(held, kind, mask))
    return held, round_of(held, "core", 1)


def widened(panel):
    total = panel.shape[0]

    def kernel(panel_ref, wide_ref):
        def widen(j, _):
            start = pl.multiple_of(j * 64, 64)
            value = panel_ref[pl.ds(start, 64), :].astype(jnp.float32)
            to = pl.multiple_of(2 * start, 128)
            wide_ref[pl.ds(to, 64, stride=2), :] = value[:, :128]
            wide_ref[pl.ds(to + 1, 64, stride=2), :] = value[:, 128:]
            return 0

        lax.fori_loop(0, total // 64, widen, 0, unroll=4)

    vmem = pl.BlockSpec(memory_space=pltpu.VMEM)
    return pl.pallas_call(
        kernel,
        in_specs=[vmem],
        out_specs=vmem,
        out_shape=pltpu.VMEM((2 * total, 128), jnp.float32),
        compiler_params=pltpu.CompilerParams(vmem_limit_bytes=1 << 20),
        cost_estimate=pl.CostEstimate(flops=0, transcendentals=0, bytes_accessed=0),
        name="widen",
    )(panel)


def gathered(node_map, place, wide, count, column, name):
    def kernel(map_ref, place_ref, wide_ref, out_ref, _, buf):
        def pair(p, _):
            def run(j, _):
                radial, axial = column(2 * p + j // 3, place_ref)
                base = ((j % 3 * RN + radial) * AN + axial) * CN
                rows = []
                for i in range(CN):
                    row = map_ref[base + i]
                    rows.append(wide_ref[pl.ds(pl.multiple_of(2 * row, 2), 2), :])
                to = pl.multiple_of(j * 2 * CN, 2 * CN)
                for i in range(CN):
                    buf[pl.ds(to + 2 * i, 2), :] = rows[i]
                return 0

            lax.fori_loop(0, 6, run, 0)
            start = pl.multiple_of(p * 2 * ROWS, 2 * ROWS)
            for half in range(2):
                out_ref[pl.ds(start, 2 * ROWS), half * 128 : half * 128 + 128] = buf[
                    pl.ds(half, 2 * ROWS, stride=2), :
                ].astype(jnp.bfloat16)
            return 0

        lax.fori_loop(0, count // 2, pair, 0)

    vmem = pl.BlockSpec(memory_space=pltpu.VMEM)
    return pl.pallas_call(
        kernel,
        in_specs=[pl.BlockSpec(memory_space=pltpu.SMEM)] * 2 + [vmem],
        out_specs=[vmem, vmem],
        out_shape=[
            jax.ShapeDtypeStruct((count * ROWS, 256), jnp.bfloat16),
            pltpu.VMEM(wide.shape, wide.dtype),
        ],
        input_output_aliases={2: 1},
        scratch_shapes=[pltpu.VMEM((4 * ROWS, 128), jnp.float32)],
        compiler_params=pltpu.CompilerParams(vmem_limit_bytes=2 << 20),
        cost_estimate=pl.CostEstimate(flops=0, transcendentals=0, bytes_accessed=0),
        name=name,
    )(node_map, place, wide)


def stressed(halos, faces, inner, modal, place, modulus):
    def kernel(*refs):
        halo_refs, face_refs, inner_refs = refs[:4], refs[4:8], refs[8:11]
        held_ref, other_ref, place_ref, modulus_ref, out_ref, modal_ref, field = refs[11:]
        harmonic, radial = pl.program_id(0), pl.program_id(1)

        def displace(ref, first, count, place):
            for start in range(first, first + count, 4):
                n = min(4, first + count - start)
                value = jnp.dot(
                    ref[start * ROWS : (start + n) * ROWS, :],
                    modal_ref[harmonic],
                    preferred_element_type=jnp.float32,
                )
                value = value.astype(jnp.bfloat16).astype(jnp.float32)
                for b in range(n):
                    r, a = place(start + b)
                    for k in range(3):
                        low = b * ROWS + k * CN
                        for t in range(2):
                            field[r, a, k, t, 8 : 8 + CN, :] = value[
                                low : low + CN, t * 128 : t * 128 + 128
                            ]

        @pl.when(jnp.logical_and(radial == 0, harmonic == 0))
        def _():
            core = place_ref[1]
            modal_ref[core] = held_ref[...]
            modal_ref[1 - core] = other_ref[...]
            zeros = jnp.zeros((8, 128), jnp.float32)

            def clear(r, _):
                for a in range(1, AN + 1):
                    for k in range(3):
                        for t in range(2):
                            field[r, a, k, t, 0:8, :] = zeros
                            field[r, a, k, t, 8 + CN : 16 + CN, :] = zeros
                return 0

            lax.fori_loop(0, 3, clear, 0)

        odd_r, odd_a = place_ref[2], place_ref[3]
        even_a = 1 - odd_a

        def radial_side(refs, s, a_is_here):
            for ref, here in ((refs[0], a_is_here), (refs[1], 1 - a_is_here)):
                pl.when(here == 1)(
                    lambda ref=ref: displace(ref, 0, 8, lambda b: (s % 3, b + 1))
                )

        def slab(s):
            if s == 0 or s == RN + 1:
                radial_side(halo_refs[:2], s, odd_r if s == 0 else 1 - odd_r)
                return
            if s == 1 or s == RN:
                radial_side(face_refs[:2], s, odd_r if s == 1 else 1 - odd_r)
            else:
                part, place = divmod(s - 2, 2)
                skip = (AN - 2) * place
                displace(inner_refs[part], skip, 6, lambda b: (s % 3, b - skip + 2))
                displace(face_refs[2], s - 1, 1, lambda b: (s % 3, 1 + (AN - 1) * even_a))
                displace(face_refs[3], s - 1, 1, lambda b: (s % 3, 1 + (AN - 1) * odd_a))
            displace(halo_refs[2], s - 1, 1, lambda b: (s % 3, (AN + 1) * even_a))
            displace(halo_refs[3], s - 1, 1, lambda b: (s % 3, (AN + 1) * odd_a))

        @pl.when(radial == 0)
        def _():
            slab(0)
            slab(1)

        for s in range(2, RN + 2):
            pl.when(radial == s - 2)(lambda s=s: slab(s))
        low, mid, high = (lax.rem(radial + i, 3) for i in range(3))

        scale = jnp.transpose(modulus_ref[0] * SCALE)
        for a in range(AN):
            for start in range(0, CN, 16):
                factor = jnp.broadcast_to(scale[start : start + 16, a : a + 1], (16, 128))
                here = slice(8 + start, 24 + start)
                after = slice(9 + start, 25 + start)
                before = slice(7 + start, 23 + start)
                for t in range(2):
                    diff = [
                        [
                            field[high, a + 1, k, t, here, :]
                            - field[low, a + 1, k, t, here, :],
                            field[mid, a + 2, k, t, here, :]
                            - field[mid, a, k, t, here, :],
                            field[mid, a + 1, k, t, after, :]
                            - field[mid, a + 1, k, t, before, :],
                        ]
                        for k in range(3)
                    ]
                    volume = (diff[0][0] + diff[1][1] + diff[2][2]) * LAME_RATIO
                    normal = [volume + diff[k][k] for k in range(3)]
                    total = (
                        (normal[0] - normal[1]) ** 2
                        + (normal[1] - normal[2]) ** 2
                        + (normal[2] - normal[0]) ** 2
                    )
                    mixed = (
                        (diff[0][1] + diff[1][0]) ** 2
                        + (diff[1][2] + diff[2][1]) ** 2
                        + (diff[0][2] + diff[2][0]) ** 2
                    )
                    total = total + 1.5 * mixed
                    root = total * lax.rsqrt(jnp.maximum(total, TINY))
                    out_ref[0, a, start : start + 16, t * 128 : t * 128 + 128] = (
                        factor * root
                    ).astype(jnp.bfloat16)

    vmem = pl.BlockSpec(memory_space=pltpu.VMEM)
    return pl.pallas_call(
        kernel,
        grid=(2, RN),
        in_specs=[vmem] * 13
        + [
            pl.BlockSpec(memory_space=pltpu.SMEM),
            pl.BlockSpec((1, AN, CN), lambda h, r: (r, 0, 0)),
        ],
        out_specs=pl.BlockSpec((1, AN, CN, 256), lambda h, r: (r, 0, 0, h)),
        out_shape=jax.ShapeDtypeStruct((RN, AN, CN, 512), jnp.bfloat16),
        scratch_shapes=[
            pltpu.VMEM((2, 256, 256), jnp.bfloat16),
            pltpu.VMEM((3, AN + 2, 3, 2, CN + 16, 128), jnp.float32),
        ],
        compiler_params=pltpu.CompilerParams(vmem_limit_bytes=16 << 20),
        name="stress",
    )(*halos, *faces, *inner, *modal, place, modulus)


def local(responses, owners, panel, node_map, modulus):
    last_r, last_a, span = RN - 1, AN - 1, AN - 2
    pairs_a = [(i, i ^ 1) for i in range(16)]
    pairs_b = [(i, i + 1 if i % 2 else i - 1) for i in range(1, 15)]
    columns = {
        "radial_a": (8, lambda b, place: (last_r * (1 - place[2]), b)),
        "radial_b": (8, lambda b, place: (last_r * place[2], b)),
        "axial_a": (8, lambda b, place: (b, last_a * (1 - place[3]))),
        "axial_b": (8, lambda b, place: (b, last_a * place[3])),
    }
    for part in range(3):
        columns[f"inner_{part}"] = (
            2 * span,
            lambda b, place, part=part: (1 + 2 * part + b // span, 1 + b % span),
        )
    wide, rows = [], {}
    radial, axial = lax.axis_index("radial"), lax.axis_index("axial")
    place = jnp.stack([radial * 16 + axial, axial % 2, radial % 2, axial % 2]).astype(jnp.int32)

    def gather(*names):
        def run(value):
            if not wide:
                wide.append(widened(lax.optimization_barrier((panel[0, 0], value))[0]))
            own = lax.optimization_barrier((node_map[0, 0], value))[0]
            for name in names:
                rows[name], wide[0] = gathered(own, place, wide[0], *columns[name], name)
            return tuple(rows[name] for name in names)

        return run

    modal = broadcast(
        responses,
        owners,
        place,
        [gather(*names) for names in WORK],
    )
    halos = [
        lax.ppermute(rows["radial_a"], "radial", pairs_a),
        lax.ppermute(rows["radial_b"], "radial", pairs_b),
        lax.ppermute(rows["axial_a"], "axial", pairs_a),
        lax.ppermute(rows["axial_b"], "axial", pairs_b),
    ]
    faces = [rows[name] for name in ("radial_a", "radial_b", "axial_a", "axial_b")]
    inner = [rows[f"inner_{part}"] for part in range(3)]
    return stressed(halos, faces, inner, modal, place, modulus)


def solution(mesh):
    return jax.shard_map(
        local,
        mesh=mesh,
        in_specs=(
            P("radial", "axial", None, None, None),
            P(),
            P("radial", "axial", None, None),
            P("radial", "axial", None),
            P("radial", "axial", None),
        ),
        out_specs=P("radial", "axial", None, None),
        check_vma=False,
    )
```

```python
import math

import jax
import jax.numpy as jnp
from jax import lax
from jax.experimental import pallas as pl
from jax.experimental.pallas import tpu as pltpu
from jax.sharding import PartitionSpec as P

RN = 8
AN = 8
CN = 64
ROWS = 3 * CN
AXES = ("radial", "axial")
POISSON = 0.3
LAME_RATIO = POISSON / (1.0 - 2.0 * POISSON)
SCALE = 1.0 / (2.0 * (1.0 + POISSON))
TINY = 1.1754944e-38


def swapped(kind, mask):
    pairs = []
    for i in range(256):
        radial, axial = divmod(i, 16)
        x, z = (axial // 2) % 2 * 2 + radial // 8, radial % 8
        y, core = axial // 4, axial % 2
        if kind == "core":
            core ^= mask
        elif kind == "z":
            z ^= mask
        elif kind == "y":
            y ^= mask
        else:
            x ^= mask
        pairs.append((i, (x % 2 * 8 + z) * 16 + y * 4 + x // 2 * 2 + core))
    return pairs


def sent(value, kind, mask):
    return lax.ppermute(value, AXES, swapped(kind, mask))


WORK = (
    (),
    ("radial_b",),
    ("radial_a",),
    ("axial_b",),
    ("axial_a",),
    ("inner_0",),
    ("inner_1",),
    ("inner_2",),
)


def added(a, b):
    def kernel(a_ref, b_ref, out_ref):
        out_ref[...] = a_ref[...] + b_ref[...]

    vmem = pl.BlockSpec(memory_space=pltpu.VMEM)
    return pl.pallas_call(
        kernel,
        in_specs=[vmem, vmem],
        out_specs=vmem,
        out_shape=jax.ShapeDtypeStruct(a.shape, a.dtype),
        compiler_params=pltpu.CompilerParams(vmem_limit_bytes=1 << 20),
        cost_estimate=pl.CostEstimate(flops=0, transcendentals=0, bytes_accessed=0),
        name="add",
    )(a, b)


def masked(responses, owners, place):
    def kernel(owners_ref, place_ref, in_ref, own_ref, other_ref, sems):
        me, core = place_ref[0], place_ref[1]
        for i, (out_ref, h) in enumerate(((other_ref, 1 - core), (own_ref, core))):

            @pl.when(owners_ref[h] == me)
            def _(out_ref=out_ref, h=h, i=i):
                copy = pltpu.make_async_copy(in_ref.at[h], out_ref, sems.at[i])
                copy.start()
                copy.wait()

            @pl.when(owners_ref[h] != me)
            def _(out_ref=out_ref):
                out_ref[...] = jnp.zeros_like(out_ref)

    smem, vmem = pl.BlockSpec(memory_space=pltpu.SMEM), pl.BlockSpec(memory_space=pltpu.VMEM)
    shape = jax.ShapeDtypeStruct(responses.shape[1:], responses.dtype)
    return pl.pallas_call(
        kernel,
        in_specs=[smem, smem, pl.BlockSpec(memory_space=pltpu.HBM)],
        out_specs=[vmem, vmem],
        out_shape=[shape, shape],
        scratch_shapes=[pltpu.SemaphoreType.DMA((2,))],
        compiler_params=pltpu.CompilerParams(vmem_limit_bytes=1 << 20),
        name="mask",
    )(owners, place, pltpu.with_memory_space_constraint(responses, pltpu.HBM))


ROUNDS = (("x", 1), ("x", 3), ("y", 1), ("y", 3), ("z", 1), ("z", 2), ("z", 6))


def broadcast(responses, owners, place, work):
    work = list(work)

    def round_of(value, kind, mask):
        value = lax.optimization_barrier(value)
        part = sent(value, kind, mask)
        done = work.pop(0)(value) if work else ()
        return lax.optimization_barrier((part, done))[0]

    held, other = masked(responses[0, 0], owners, place)
    held = added(held, round_of(other, "core", 1))
    for kind, mask in ROUNDS:
        held = added(held, round_of(held, kind, mask))
    return held, round_of(held, "core", 1)


def widened(panel):
    total = panel.shape[0]
    chunk = total // 8

    def kernel(panel_ref, wide_ref, buf, sems):
        def fetch(i):
            return pltpu.make_async_copy(
                panel_ref.at[pl.ds(i * chunk, chunk), :], buf.at[i], sems.at[i]
            )

        for i in range(8):
            fetch(i).start()
        for i in range(8):
            fetch(i).wait()

            def widen(j, _, i=i):
                start = pl.multiple_of(j * 64, 64)
                value = buf[i, pl.ds(start, 64), :].astype(jnp.float32)
                to = pl.multiple_of(2 * (i * chunk + start), 128)
                wide_ref[pl.ds(to, 64, stride=2), :] = value[:, :128]
                wide_ref[pl.ds(to + 1, 64, stride=2), :] = value[:, 128:]
                return 0

            lax.fori_loop(0, chunk // 64, widen, 0, unroll=4)

    vmem = pl.BlockSpec(memory_space=pltpu.VMEM)
    return pl.pallas_call(
        kernel,
        in_specs=[pl.BlockSpec(memory_space=pltpu.HBM)],
        out_specs=vmem,
        out_shape=pltpu.VMEM((2 * total, 128), jnp.float32),
        scratch_shapes=[
            pltpu.VMEM((8, chunk, 256), jnp.bfloat16),
            pltpu.SemaphoreType.DMA((8,)),
        ],
        compiler_params=pltpu.CompilerParams(vmem_limit_bytes=8 << 20),
        cost_estimate=pl.CostEstimate(flops=0, transcendentals=0, bytes_accessed=0),
        name="widen",
    )(pltpu.with_memory_space_constraint(panel, pltpu.HBM))


def gathered(node_map, place, wide, count, column, name):
    def kernel(map_ref, place_ref, wide_ref, out_ref, _, buf):
        def pair(p, _):
            for j in range(6):
                radial, axial = column(2 * p + j // 3, place_ref)
                base = ((j % 3 * RN + radial) * AN + axial) * CN
                rows = []
                for i in range(CN):
                    row = map_ref[base + i]
                    rows.append(wide_ref[pl.ds(pl.multiple_of(2 * row, 2), 2), :])
                for i in range(CN):
                    buf[j * 2 * CN + 2 * i : j * 2 * CN + 2 * i + 2, :] = rows[i]
            start = pl.multiple_of(p * 2 * ROWS, 2 * ROWS)
            for half in range(2):
                out_ref[pl.ds(start, 2 * ROWS), half * 128 : half * 128 + 128] = buf[
                    pl.ds(half, 2 * ROWS, stride=2), :
                ].astype(jnp.bfloat16)
            return 0

        lax.fori_loop(0, count // 2, pair, 0)

    vmem = pl.BlockSpec(memory_space=pltpu.VMEM)
    return pl.pallas_call(
        kernel,
        in_specs=[pl.BlockSpec(memory_space=pltpu.SMEM)] * 2 + [vmem],
        out_specs=[vmem, vmem],
        out_shape=[
            jax.ShapeDtypeStruct((count * ROWS, 256), jnp.bfloat16),
            pltpu.VMEM(wide.shape, wide.dtype),
        ],
        input_output_aliases={2: 1},
        scratch_shapes=[pltpu.VMEM((4 * ROWS, 128), jnp.float32)],
        compiler_params=pltpu.CompilerParams(vmem_limit_bytes=2 << 20),
        cost_estimate=pl.CostEstimate(flops=0, transcendentals=0, bytes_accessed=0),
        name=name,
    )(node_map, place, wide)


def stressed(halos, faces, inner, modal, place, modulus):
    def kernel(*refs):
        halo_refs, face_refs, inner_refs = refs[:4], refs[4:8], refs[8:11]
        held_ref, other_ref, place_ref, modulus_ref, out_ref, modal_ref, field = refs[11:]
        harmonic, radial = pl.program_id(0), pl.program_id(1)

        def displace(ref, first, count, place):
            for start in range(first, first + count, 2):
                n = min(2, first + count - start)
                value = jnp.dot(
                    ref[start * ROWS : (start + n) * ROWS, :],
                    modal_ref[harmonic],
                    preferred_element_type=jnp.float32,
                )
                value = value.astype(jnp.bfloat16).astype(jnp.float32)
                for b in range(n):
                    r, a = place(start + b)
                    for k in range(3):
                        low = b * ROWS + k * CN
                        for t in range(2):
                            field[r, a, k, t, 8 : 8 + CN, :] = value[
                                low : low + CN, t * 128 : t * 128 + 128
                            ]

        @pl.when(jnp.logical_and(radial == 0, harmonic == 0))
        def _():
            core = place_ref[1]
            modal_ref[core] = held_ref[...]
            modal_ref[1 - core] = other_ref[...]
            zeros = jnp.zeros((8, 128), jnp.float32)

            def clear(r, _):
                for a in range(1, AN + 1):
                    for k in range(3):
                        for t in range(2):
                            field[r, a, k, t, 0:8, :] = zeros
                            field[r, a, k, t, 8 + CN : 16 + CN, :] = zeros
                return 0

            lax.fori_loop(1, RN + 1, clear, 0)

        odd_r, odd_a = place_ref[2], place_ref[3]
        even_r, even_a = 1 - odd_r, 1 - odd_a

        @pl.when(radial == 0)
        def _():
            inner = AN - 2
            for i in range(3):
                displace(inner_refs[i], 0, 2 * inner, lambda b: (2 + 2 * i + b // inner, 2 + b % inner))
            displace(face_refs[0], 0, 8, lambda b: (1 + (RN - 1) * even_r, b + 1))
            displace(face_refs[1], 0, 8, lambda b: (1 + (RN - 1) * odd_r, b + 1))
            displace(face_refs[2], 1, 6, lambda b: (b + 1, 1 + (AN - 1) * even_a))
            displace(face_refs[3], 1, 6, lambda b: (b + 1, 1 + (AN - 1) * odd_a))
            displace(halo_refs[0], 0, 8, lambda b: ((RN + 1) * even_r, b + 1))
            displace(halo_refs[1], 0, 8, lambda b: ((RN + 1) * odd_r, b + 1))
            displace(halo_refs[2], 0, 8, lambda b: (b + 1, (AN + 1) * even_a))
            displace(halo_refs[3], 0, 8, lambda b: (b + 1, (AN + 1) * odd_a))

        low, mid, high = radial, radial + 1, radial + 2
        scale = jnp.transpose(modulus_ref[0] * SCALE)
        for t in range(2):
            for start in range(0, CN, 16):
                here = slice(8 + start, 24 + start)
                after = slice(9 + start, 25 + start)
                before = slice(7 + start, 23 + start)
                left = [field[mid, 0, k, t, here, :] for k in range(3)]
                centre = [field[mid, 1, k, t, here, :] for k in range(3)]
                for a in range(AN):
                    right = [field[mid, a + 2, k, t, here, :] for k in range(3)]
                    diff = [
                        [
                            field[high, a + 1, k, t, here, :] - field[low, a + 1, k, t, here, :],
                            right[k] - left[k],
                            field[mid, a + 1, k, t, after, :] - field[mid, a + 1, k, t, before, :],
                        ]
                        for k in range(3)
                    ]
                    left, centre = centre, right
                    volume = (diff[0][0] + diff[1][1] + diff[2][2]) * LAME_RATIO
                    normal = [volume + diff[k][k] for k in range(3)]
                    first, second = normal[0] - normal[1], normal[1] - normal[2]
                    total = first * first + second * (first + second)
                    mixed = (
                        (diff[0][1] + diff[1][0]) ** 2
                        + (diff[1][2] + diff[2][1]) ** 2
                        + (diff[0][2] + diff[2][0]) ** 2
                    )
                    total = total + 0.75 * mixed
                    root = total * lax.rsqrt(jnp.maximum(total, TINY))
                    out_ref[0, a, start : start + 16, t * 128 : t * 128 + 128] = (
                        jnp.broadcast_to(scale[start : start + 16, a : a + 1], (16, 128)) * root
                    ).astype(jnp.bfloat16)

    vmem = pl.BlockSpec(memory_space=pltpu.VMEM)
    return pl.pallas_call(
        kernel,
        grid=(2, RN),
        in_specs=[vmem] * 13
        + [
            pl.BlockSpec(memory_space=pltpu.SMEM),
            pl.BlockSpec((1, AN, CN), lambda h, r: (r, 0, 0)),
        ],
        out_specs=pl.BlockSpec((1, AN, CN, 256), lambda h, r: (r, 0, 0, h)),
        out_shape=jax.ShapeDtypeStruct((RN, AN, CN, 512), jnp.bfloat16),
        scratch_shapes=[
            pltpu.VMEM((2, 256, 256), jnp.bfloat16),
            pltpu.VMEM((RN + 2, AN + 2, 3, 2, CN + 16, 128), jnp.float32),
        ],
        compiler_params=pltpu.CompilerParams(vmem_limit_bytes=32 << 20),
        name="stress",
    )(*halos, *faces, *inner, *modal, place, modulus)


def local(responses, owners, panel, node_map, modulus):
    last_r, last_a, span = RN - 1, AN - 1, AN - 2
    pairs_a = [(i, i ^ 1) for i in range(16)]
    pairs_b = [(i, i + 1 if i % 2 else i - 1) for i in range(1, 15)]
    columns = {
        "radial_a": (8, lambda b, place: (last_r * (1 - place[2]), b)),
        "radial_b": (8, lambda b, place: (last_r * place[2], b)),
        "axial_a": (8, lambda b, place: (b, last_a * (1 - place[3]))),
        "axial_b": (8, lambda b, place: (b, last_a * place[3])),
    }
    for part in range(3):
        columns[f"inner_{part}"] = (
            2 * span,
            lambda b, place, part=part: (1 + 2 * part + b // span, 1 + b % span),
        )
    wide, rows = [], {}
    radial, axial = lax.axis_index("radial"), lax.axis_index("axial")
    place = jnp.stack([radial * 16 + axial, axial % 2, radial % 2, axial % 2]).astype(jnp.int32)

    def gather(*names):
        def run(value):
            if not wide:
                wide.append(widened(lax.optimization_barrier((panel[0, 0], value))[0]))
            own = lax.optimization_barrier((node_map[0, 0], value))[0]
            for name in names:
                rows[name], wide[0] = gathered(own, place, wide[0], *columns[name], name)
            return tuple(rows[name] for name in names)

        return run

    modal = broadcast(
        responses,
        owners,
        place,
        [gather(*names) for names in WORK],
    )
    halos = [
        lax.ppermute(rows["radial_a"], "radial", pairs_a),
        lax.ppermute(rows["radial_b"], "radial", pairs_b),
        lax.ppermute(rows["axial_a"], "axial", pairs_a),
        lax.ppermute(rows["axial_b"], "axial", pairs_b),
    ]
    faces = [rows[name] for name in ("radial_a", "radial_b", "axial_a", "axial_b")]
    inner = [rows[f"inner_{part}"] for part in range(3)]
    return stressed(halos, faces, inner, modal, place, modulus)


def solution(mesh):
    return jax.shard_map(
        local,
        mesh=mesh,
        in_specs=(
            P("radial", "axial", None, None, None),
            P(),
            P("radial", "axial", None, None),
            P("radial", "axial", None),
            P("radial", "axial", None),
        ),
        out_specs=P("radial", "axial", None, None),
        check_vma=False,
    )
```

```python
import math

import jax
import jax.numpy as jnp
from jax import lax
from jax.experimental import pallas as pl
from jax.experimental.pallas import tpu as pltpu
from jax.sharding import PartitionSpec as P

RN = 8
AN = 8
CN = 64
ROWS = 3 * CN
AXES = ("radial", "axial")
POISSON = 0.3
LAME_RATIO = POISSON / (1.0 - 2.0 * POISSON)
SCALE = 1.0 / (2.0 * (1.0 + POISSON))
TINY = 1.1754944e-38


def swapped(kind, mask):
    pairs = []
    for i in range(256):
        radial, axial = divmod(i, 16)
        x, z = (axial // 2) % 2 * 2 + radial // 8, radial % 8
        y, core = axial // 4, axial % 2
        if kind == "core":
            core ^= mask
        elif kind == "z":
            z ^= mask
        elif kind == "y":
            y ^= mask
        else:
            x ^= mask
        pairs.append((i, (x % 2 * 8 + z) * 16 + y * 4 + x // 2 * 2 + core))
    return pairs


def sent(value, kind, mask):
    return lax.ppermute(value, AXES, swapped(kind, mask))


SETTLED = 5
WORK = (
    (),
    ("radial_b",),
    ("radial_a",),
    ("axial_b",),
    ("inner_0",),
    ("axial_a",),
    ("inner_1",),
    ("inner_2",),
)


def added(a, b):
    def kernel(a_ref, b_ref, out_ref):
        out_ref[...] = a_ref[...] + b_ref[...]

    vmem = pl.BlockSpec(memory_space=pltpu.VMEM)
    return pl.pallas_call(
        kernel,
        in_specs=[vmem, vmem],
        out_specs=vmem,
        out_shape=jax.ShapeDtypeStruct(a.shape, a.dtype),
        compiler_params=pltpu.CompilerParams(vmem_limit_bytes=1 << 20),
        cost_estimate=pl.CostEstimate(flops=0, transcendentals=0, bytes_accessed=0),
        name="add",
    )(a, b)


def masked(responses, owners, place):
    def kernel(owners_ref, place_ref, in_ref, own_ref, other_ref, sems):
        me, core = place_ref[0], place_ref[1]
        for i, (out_ref, h) in enumerate(((other_ref, 1 - core), (own_ref, core))):

            @pl.when(owners_ref[h] == me)
            def _(out_ref=out_ref, h=h, i=i):
                copy = pltpu.make_async_copy(in_ref.at[h], out_ref, sems.at[i])
                copy.start()
                copy.wait()

            @pl.when(owners_ref[h] != me)
            def _(out_ref=out_ref):
                out_ref[...] = jnp.zeros_like(out_ref)

    smem, vmem = pl.BlockSpec(memory_space=pltpu.SMEM), pl.BlockSpec(memory_space=pltpu.VMEM)
    shape = jax.ShapeDtypeStruct(responses.shape[1:], responses.dtype)
    return pl.pallas_call(
        kernel,
        in_specs=[smem, smem, pl.BlockSpec(memory_space=pltpu.HBM)],
        out_specs=[vmem, vmem],
        out_shape=[shape, shape],
        scratch_shapes=[pltpu.SemaphoreType.DMA((2,))],
        compiler_params=pltpu.CompilerParams(vmem_limit_bytes=1 << 20),
        name="mask",
    )(owners, place, pltpu.with_memory_space_constraint(responses, pltpu.HBM))


ROUNDS = (("x", 1), ("x", 3), ("y", 1), ("y", 3), ("z", 1), ("z", 2), ("z", 6))


def broadcast(responses, owners, place, work, settle):
    work = list(work)

    def round_of(value, kind, mask):
        value = lax.optimization_barrier(value)
        part = sent(value, kind, mask)
        done = work.pop(0)(value) if work else ()
        return lax.optimization_barrier((part, done))[0]

    held, other = masked(responses[0, 0], owners, place)
    held = added(held, round_of(other, "core", 1))
    for number, (kind, mask) in enumerate(ROUNDS):
        if number == SETTLED:
            held = settle(held)
        held = added(held, round_of(held, kind, mask))
    return held, round_of(held, "core", 1)


def widened(panel):
    total = panel.shape[0]
    chunk = total // 8

    def kernel(panel_ref, wide_ref, buf, sems):
        def fetch(i):
            return pltpu.make_async_copy(
                panel_ref.at[pl.ds(i * chunk, chunk), :], buf.at[i], sems.at[i]
            )

        for i in range(8):
            fetch(i).start()
        for i in range(8):
            fetch(i).wait()

            def widen(j, _, i=i):
                start = pl.multiple_of(j * 64, 64)
                value = buf[i, pl.ds(start, 64), :].astype(jnp.float32)
                to = pl.multiple_of(2 * (i * chunk + start), 128)
                wide_ref[pl.ds(to, 64, stride=2), :] = value[:, :128]
                wide_ref[pl.ds(to + 1, 64, stride=2), :] = value[:, 128:]
                return 0

            lax.fori_loop(0, chunk // 64, widen, 0, unroll=4)

    vmem = pl.BlockSpec(memory_space=pltpu.VMEM)
    return pl.pallas_call(
        kernel,
        in_specs=[pl.BlockSpec(memory_space=pltpu.HBM)],
        out_specs=vmem,
        out_shape=pltpu.VMEM((2 * total, 128), jnp.float32),
        scratch_shapes=[
            pltpu.VMEM((8, chunk, 256), jnp.bfloat16),
            pltpu.SemaphoreType.DMA((8,)),
        ],
        compiler_params=pltpu.CompilerParams(vmem_limit_bytes=8 << 20),
        cost_estimate=pl.CostEstimate(flops=0, transcendentals=0, bytes_accessed=0),
        name="widen",
    )(pltpu.with_memory_space_constraint(panel, pltpu.HBM))


def gathered(node_map, place, wide, count, column, name):
    def kernel(map_ref, place_ref, wide_ref, out_ref, _, buf):
        def pair(p, _):
            for j in range(6):
                radial, axial = column(2 * p + j // 3, place_ref)
                base = ((j % 3 * RN + radial) * AN + axial) * CN
                rows = []
                for i in range(CN):
                    row = map_ref[base + i]
                    rows.append(wide_ref[pl.ds(pl.multiple_of(2 * row, 2), 2), :])
                for i in range(CN):
                    buf[j * 2 * CN + 2 * i : j * 2 * CN + 2 * i + 2, :] = rows[i]
            start = pl.multiple_of(p * 2 * ROWS, 2 * ROWS)
            for half in range(2):
                out_ref[pl.ds(start, 2 * ROWS), half * 128 : half * 128 + 128] = buf[
                    pl.ds(half, 2 * ROWS, stride=2), :
                ].astype(jnp.bfloat16)
            return 0

        lax.fori_loop(0, count // 2, pair, 0)

    vmem = pl.BlockSpec(memory_space=pltpu.VMEM)
    return pl.pallas_call(
        kernel,
        in_specs=[pl.BlockSpec(memory_space=pltpu.SMEM)] * 2 + [vmem],
        out_specs=[vmem, vmem],
        out_shape=[
            jax.ShapeDtypeStruct((count * ROWS, 256), jnp.bfloat16),
            pltpu.VMEM(wide.shape, wide.dtype),
        ],
        input_output_aliases={2: 1},
        scratch_shapes=[pltpu.VMEM((4 * ROWS, 128), jnp.float32)],
        compiler_params=pltpu.CompilerParams(vmem_limit_bytes=2 << 20),
        cost_estimate=pl.CostEstimate(flops=0, transcendentals=0, bytes_accessed=0),
        name=name,
    )(node_map, place, wide)


def stressed(halos, faces, inner, modal, place, modulus):
    def kernel(*refs):
        halo_refs, face_refs, inner_refs = refs[:4], refs[4:8], refs[8:11]
        held_ref, other_ref, place_ref, modulus_ref, out_ref, modal_ref, field = refs[11:]
        harmonic, radial = pl.program_id(0), pl.program_id(1)

        def displace(ref, first, count, place):
            for start in range(first, first + count, 2):
                n = min(2, first + count - start)
                value = jnp.dot(
                    ref[start * ROWS : (start + n) * ROWS, :],
                    modal_ref[harmonic],
                    preferred_element_type=jnp.float32,
                )
                value = value.astype(jnp.bfloat16).astype(jnp.float32)
                for b in range(n):
                    r, a = place(start + b)
                    for k in range(3):
                        low = b * ROWS + k * CN
                        for t in range(2):
                            field[r, a, k, t, 8 : 8 + CN, :] = value[
                                low : low + CN, t * 128 : t * 128 + 128
                            ]

        @pl.when(jnp.logical_and(radial == 0, harmonic == 0))
        def _():
            core = place_ref[1]
            modal_ref[core] = held_ref[...]
            modal_ref[1 - core] = other_ref[...]
            zeros = jnp.zeros((8, 128), jnp.float32)

            def clear(r, _):
                for a in range(1, AN + 1):
                    for k in range(3):
                        for t in range(2):
                            field[r, a, k, t, 0:8, :] = zeros
                            field[r, a, k, t, 8 + CN : 16 + CN, :] = zeros
                return 0

            lax.fori_loop(1, RN + 1, clear, 0)

        odd_r, odd_a = place_ref[2], place_ref[3]
        even_r, even_a = 1 - odd_r, 1 - odd_a

        @pl.when(radial == 0)
        def _():
            inner = AN - 2
            for i in range(3):
                displace(inner_refs[i], 0, 2 * inner, lambda b: (2 + 2 * i + b // inner, 2 + b % inner))
            displace(face_refs[0], 0, 8, lambda b: (1 + (RN - 1) * even_r, b + 1))
            displace(face_refs[1], 0, 8, lambda b: (1 + (RN - 1) * odd_r, b + 1))
            displace(face_refs[2], 1, 6, lambda b: (b + 1, 1 + (AN - 1) * even_a))
            displace(face_refs[3], 1, 6, lambda b: (b + 1, 1 + (AN - 1) * odd_a))
            displace(halo_refs[0], 0, 8, lambda b: ((RN + 1) * even_r, b + 1))
            displace(halo_refs[1], 0, 8, lambda b: ((RN + 1) * odd_r, b + 1))
            displace(halo_refs[2], 0, 8, lambda b: (b + 1, (AN + 1) * even_a))
            displace(halo_refs[3], 0, 8, lambda b: (b + 1, (AN + 1) * odd_a))

        low, mid, high = radial, radial + 1, radial + 2
        scale = jnp.transpose(modulus_ref[0] * SCALE)
        for t in range(2):
            for start in range(0, CN, 16):
                here = slice(8 + start, 24 + start)
                after = slice(9 + start, 25 + start)
                before = slice(7 + start, 23 + start)
                left = [field[mid, 0, k, t, here, :] for k in range(3)]
                centre = [field[mid, 1, k, t, here, :] for k in range(3)]
                for a in range(AN):
                    right = [field[mid, a + 2, k, t, here, :] for k in range(3)]
                    diff = [
                        [
                            field[high, a + 1, k, t, here, :] - field[low, a + 1, k, t, here, :],
                            right[k] - left[k],
                            field[mid, a + 1, k, t, after, :] - field[mid, a + 1, k, t, before, :],
                        ]
                        for k in range(3)
                    ]
                    left, centre = centre, right
                    volume = (diff[0][0] + diff[1][1] + diff[2][2]) * LAME_RATIO
                    normal = [volume + diff[k][k] for k in range(3)]
                    first, second = normal[0] - normal[1], normal[1] - normal[2]
                    total = first * first + second * (first + second)
                    mixed = (
                        (diff[0][1] + diff[1][0]) ** 2
                        + (diff[1][2] + diff[2][1]) ** 2
                        + (diff[0][2] + diff[2][0]) ** 2
                    )
                    total = total + 0.75 * mixed
                    root = total * lax.rsqrt(jnp.maximum(total, TINY))
                    out_ref[0, a, start : start + 16, t * 128 : t * 128 + 128] = (
                        jnp.broadcast_to(scale[start : start + 16, a : a + 1], (16, 128)) * root
                    ).astype(jnp.bfloat16)

    vmem = pl.BlockSpec(memory_space=pltpu.VMEM)
    return pl.pallas_call(
        kernel,
        grid=(2, RN),
        in_specs=[vmem] * 13
        + [
            pl.BlockSpec(memory_space=pltpu.SMEM),
            pl.BlockSpec((1, AN, CN), lambda h, r: (r, 0, 0)),
        ],
        out_specs=pl.BlockSpec((1, AN, CN, 256), lambda h, r: (r, 0, 0, h)),
        out_shape=jax.ShapeDtypeStruct((RN, AN, CN, 512), jnp.bfloat16),
        scratch_shapes=[
            pltpu.VMEM((2, 256, 256), jnp.bfloat16),
            pltpu.VMEM((RN + 2, AN + 2, 3, 2, CN + 16, 128), jnp.float32),
        ],
        compiler_params=pltpu.CompilerParams(vmem_limit_bytes=32 << 20),
        name="stress",
    )(*halos, *faces, *inner, *modal, place, modulus)


def local(responses, owners, panel, node_map, modulus):
    last_r, last_a, span = RN - 1, AN - 1, AN - 2
    pairs_a = [(i, i ^ 1) for i in range(16)]
    pairs_b = [(i, i + 1 if i % 2 else i - 1) for i in range(1, 15)]
    columns = {
        "radial_a": (8, lambda b, place: (last_r * (1 - place[2]), b)),
        "radial_b": (8, lambda b, place: (last_r * place[2], b)),
        "axial_a": (8, lambda b, place: (b, last_a * (1 - place[3]))),
        "axial_b": (8, lambda b, place: (b, last_a * place[3])),
    }
    for part in range(3):
        columns[f"inner_{part}"] = (
            2 * span,
            lambda b, place, part=part: (1 + 2 * part + b // span, 1 + b % span),
        )
    wide, rows = [], {}
    radial, axial = lax.axis_index("radial"), lax.axis_index("axial")
    place = jnp.stack([radial * 16 + axial, axial % 2, radial % 2, axial % 2]).astype(jnp.int32)

    def gather(*names):
        def run(value):
            if not wide:
                wide.append(widened(lax.optimization_barrier((panel[0, 0], value))[0]))
            own = lax.optimization_barrier((node_map[0, 0], value))[0]
            for name in names:
                rows[name], wide[0] = gathered(own, place, wide[0], *columns[name], name)
            return tuple(rows[name] for name in names)

        return run

    halos = {}

    def settle(value):
        for name, pairs in (("radial_a", pairs_a), ("radial_b", pairs_b)):
            halos[name] = lax.ppermute(rows[name], "radial", pairs)
        value, halos["radial_a"], halos["radial_b"] = lax.optimization_barrier(
            (value, halos["radial_a"], halos["radial_b"])
        )
        return value

    modal = broadcast(
        responses,
        owners,
        place,
        [gather(*names) for names in WORK],
        settle,
    )
    for name, pairs in (("axial_a", pairs_a), ("axial_b", pairs_b)):
        halos[name] = lax.ppermute(rows[name], "axial", pairs)
    halos = [halos[name] for name in ("radial_a", "radial_b", "axial_a", "axial_b")]
    faces = [rows[name] for name in ("radial_a", "radial_b", "axial_a", "axial_b")]
    inner = [rows[f"inner_{part}"] for part in range(3)]
    return stressed(halos, faces, inner, modal, place, modulus)


def solution(mesh):
    return jax.shard_map(
        local,
        mesh=mesh,
        in_specs=(
            P("radial", "axial", None, None, None),
            P(),
            P("radial", "axial", None, None),
            P("radial", "axial", None),
            P("radial", "axial", None),
        ),
        out_specs=P("radial", "axial", None, None),
        check_vma=False,
    )
```
